256 devices in a mesh: outer: 16 (over x, z_hi), dp: 8 (over y, z_lo), mp: 2 (over core).
Axes of the slice: x: 4, y: 4, z: 8 (z_hi: 4, z_lo: 2; z = z_hi * 2 + z_lo), core: 2. Of those that a mesh axis runs over, the one named last changes fastest.
Arguments:
- step_index: int32 [], replicated, may hold values from 0 to 4095
- token_ids: int32 [16, 4096], P('outer', 'dp'), may hold values from 0 to 128255, as said below
- features: bfloat16 [16, 4096, 4096], P('outer', 'dp'), may hold values from -6 to 6
- cotangent: bfloat16 [16, 4096, 2048], P('outer', 'dp', 'mp'), may hold values from -6 to 6
- weight: float32 [16, 4096, 2048], P('outer', 'dp', 'mp'), may hold values from -0.09375 to 0.09375
- momentum: float32 [16, 4096, 2048], P('outer', 'dp', 'mp'), may hold values from -0.3 to 0.3
Outputs:
- input_grad: bfloat16 [16, 4096, 4096], P('outer', 'dp')
- new_weight: float32 [16, 4096, 2048], P('outer', 'dp', 'mp')
- new_momentum: float32 [16, 4096, 2048], P('outer', 'dp', 'mp')
The draws below stay inside these ranges and needn't reach their ends.
Inputs may be any that keep to these rules, and one draw needn't show every extreme that they name: `token_ids`: the id 128004 marks padding at the end of some blocks of 512 tokens; a quarter of the tokens or so are padding.
All inputs are finite; a program needn't handle non-finite values.
Results may differ from the reference program's by a relative error of at most 0.0049.
Values may be sent and summed in bfloat16 or wider, within the bound.
A program may use at most 128 MiB of HBM per device.

```python
import jax
import jax.numpy as jnp
from jax import lax

D = 4096
VOCAB = 128256
TOK_DEV = 512
KVW = 2048
POD_TOKENS = 4096
N_OUTER = 16


def draw_token_ids(key, part):
    key_ids, key_tail = jax.random.split(key)
    blocks = POD_TOKENS // TOK_DEV
    token_vals = jax.random.randint(key_ids, (N_OUTER, blocks, TOK_DEV), 0, VOCAB, dtype=jnp.int32)
    pad_len = jax.random.randint(key_tail, (N_OUTER, blocks, 1), 0, TOK_DEV // 2 + 1, dtype=jnp.int32)
    offset = jnp.arange(TOK_DEV, dtype=jnp.int32)[None, None, :]
    padded = offset >= TOK_DEV - pad_len
    token_vals = jnp.where(padded, jnp.int32(128004), token_vals)
    return token_vals.reshape(N_OUTER, POD_TOKENS)


def steps_of(key, dims, cuts, smallest, largest):
    factor_of, own = 1.0, jax.random.fold_in(key, 6)
    for dim, shards_of in cuts:
        steps = jnp.exp(jax.random.uniform(jax.random.fold_in(own, dim), (shards_of,), jnp.float32, smallest / len(cuts), largest / len(cuts)))
        factor_of = factor_of * jnp.repeat(steps, dims[dim] // shards_of).reshape([-1 if axis == dim else 1 for axis in range(len(dims))])
    return factor_of


def normal_values(key, extent, width, bound, cuts=(), kind=jnp.bfloat16):
    entries = width * jax.random.normal(key, extent, jnp.float32)
    if cuts:
        entries = entries * steps_of(key, extent, cuts, -0.22, 0.18)
    return jnp.clip(entries, -bound, bound).astype(kind)


def setup_inputs(seed: int = 0) -> dict:
    arg_keys = jax.random.split(jax.random.key(seed), 7)
    return {
        "step_index": jax.random.randint(arg_keys[0], (), 0, 4096).astype(jnp.int32),
        "token_ids": draw_token_ids(jax.random.fold_in(arg_keys[6], 71), 0),
        "features": normal_values(arg_keys[2], (N_OUTER, POD_TOKENS, D), 1.0, 6.0, ((0, 16), (1, 8))),
        "cotangent": normal_values(arg_keys[3], (N_OUTER, POD_TOKENS, KVW), 1.0, 6.0, ((0, 16), (1, 8), (2, 2))),
        "weight": normal_values(arg_keys[4], (N_OUTER, D, KVW), D ** -0.5, 0.09375, ((0, 16), (1, 8), (2, 2)), jnp.float32),
        "momentum": normal_values(arg_keys[5], (N_OUTER, D, KVW), 0.05, 0.3, ((0, 16), (1, 8), (2, 2)), jnp.float32),
    }


pad_token = 128004
peak_rate = 0.1
warm_steps = 4096.0
momentum_keep = 0.9


def reference(step_index, token_ids, features, cotangent, weight, momentum):
    keep_mask = (token_ids != pad_token)[..., None]
    masked = jnp.where(keep_mask, cotangent, jnp.zeros_like(cotangent))
    weight_half = weight.astype(jnp.bfloat16)

    def one_pod(pod_args):
        pod_x, pod_cot, pod_w = pod_args
        gradient = jnp.dot(pod_x.T, pod_cot, preferred_element_type=jnp.float32)
        input_grad = jnp.dot(pod_cot, pod_w.T, preferred_element_type=jnp.float32).astype(jnp.bfloat16)
        return gradient, input_grad

    gradients, input_grads = lax.map(one_pod, (features, masked, weight_half))
    gradients = gradients / POD_TOKENS
    rate = peak_rate * (step_index + 1).astype(jnp.float32) / warm_steps
    velocity = momentum_keep * momentum + gradients
    stepped = weight - rate * velocity
    bit_count = N_OUTER.bit_length() - 1
    shift_by = (step_index % bit_count).astype(jnp.int32)
    partner = jnp.bitwise_xor(jnp.arange(N_OUTER, dtype=jnp.int32), jnp.left_shift(jnp.ones((), jnp.int32), shift_by))
    new_weight = 0.5 * (stepped + stepped[partner])
    new_momentum = 0.5 * (velocity + velocity[partner])
    return input_grads, new_weight, new_momentum
```

```python
import functools

import jax
import jax.numpy as jnp
from jax import lax
from jax.experimental import pallas as pl
from jax.experimental.pallas import tpu as pltpu
from jax.sharding import PartitionSpec as P

pad_token = 128004
peak_rate = 0.1
warm_steps = 4096.0
momentum_keep = 0.9

MESH = pl.DeviceIdType.MESH
BF16 = jnp.bfloat16
F32 = jnp.float32
NY = 4
NX = 4


def body(
    bit,
    rate_ref,
    feat,
    masked,
    whalf,
    weight,
    momentum,
    grad_out,
    w_out,
    v_out,
    m_buf,
    f_buf,
    ft_buf,
    w_pair,
    rs_send,
    rs_recv,
    g_own,
    w_own,
    v_own,
    w_peer,
    v_send,
    v_peer,
    i_keep,
    i_send,
    i_recv,
    o_fin,
    o_recv,
    loc,
    snd,
    rcv,
):
    outer, dp, c = lax.axis_index("outer"), lax.axis_index("dp"), lax.axis_index("mp")
    x, zh = outer // NX, outer % NX
    y, zl = dp // 2, dp % 2
    tok, hw = masked.shape
    half = tok // 2
    blk = whalf.shape[0]
    nk = f_buf.shape[0]
    sub = f_buf.shape[2]
    nq = nk // 2

    def at_y(step):
        return (outer, ((y + step + NY) % NY) * 2 + zl, c)

    z_peer = (outer, y * 2 + 1 - zl, c)
    core_peer = (outer, dp, 1 - c)
    if bit == 0:
        other = x * 4 + zh + 1 - 2 * (zh % 2)
    elif bit == 1:
        other = x * 4 + (zh + 2) % 4
    elif bit == 2:
        other = (x + 1 - 2 * (x % 2)) * 4 + zh
    else:
        other = ((x + 2) % 4) * 4 + zh
    peer = (other, dp, c)

    count = {"loc": 0, "rem": 0}

    def local(src, dst):
        i = count["loc"]
        count["loc"] += 1
        copy = pltpu.make_async_copy(src, dst, loc.at[i])
        copy.start()
        return copy

    pending = []

    def remote(src, dst, to):
        i = count["rem"]
        count["rem"] += 1
        copy = pltpu.make_async_remote_copy(
            src_ref=src,
            dst_ref=dst,
            send_sem=snd.at[i],
            recv_sem=rcv.at[i],
            device_id=to,
            device_id_type=MESH,
        )
        copy.start()
        pending.append(copy)
        return copy

    in_m = local(masked, m_buf.at[pl.ds(0, tok)])
    in_w = local(whalf, w_pair.at[zl])

    barrier = pltpu.get_barrier_semaphore()
    partners = (at_y(1), at_y(-1), at_y(2), z_peer, core_peer, peer)
    for to in partners:
        pl.semaphore_signal(barrier, inc=1, device_id=to, device_id_type=MESH)
    pl.semaphore_wait(barrier, len(partners))

    lo, hi = pl.ds(0, half), pl.ds(half, half)

    def rows(r, part):
        return pl.ds(r * tok + part * half, half)

    up_a = remote(masked.at[lo], m_buf.at[rows(3, 0)], at_y(1))
    dn_b = remote(masked.at[hi], m_buf.at[rows(1, 1)], at_y(-1))
    up_b = remote(masked.at[hi], m_buf.at[rows(3, 1)], at_y(1))
    dn_a = remote(masked.at[lo], m_buf.at[rows(1, 0)], at_y(-1))
    pair = remote(whalf, w_pair.at[zl], z_peer)
    w_swap = remote(whalf, w_peer, peer)

    def columns(ychip, k):
        j = (1 - zl) if k < nq else zl
        return pl.ds(pl.multiple_of(ychip * 2 * blk + j * blk + (k % nq) * sub, sub), sub)

    in_f = [local(feat.at[:, columns(y, k)], f_buf.at[k, pl.ds(0, tok)]) for k in range(nk)]
    in_v = local(momentum, v_own)
    in_wf = local(weight, w_own)

    up_a.wait_recv()
    fwd_up = remote(m_buf.at[rows(3, 0)], m_buf.at[rows(2, 0)], at_y(1))
    dn_b.wait_recv()
    fwd_dn = remote(m_buf.at[rows(1, 1)], m_buf.at[rows(2, 1)], at_y(-1))

    mine = pl.ds(pl.multiple_of(c * half, half), half)

    def f_rows(r):
        return pl.ds(pl.multiple_of(r * tok + c * half, half), half)

    f_in = {}
    for k in range(nk):
        for step, slot in ((1, 3), (-1, 1), (2, 2)):
            f_in[k, slot] = remote(
                feat.at[mine, columns((y + step + NY) % NY, k)],
                f_buf.at[k, f_rows(slot)],
                at_y(step),
            )

    nt = blk // 2

    def partial_terms(r):
        def one(t, carry):
            j, n = t // 2, t % 2
            part = lax.dot_general(
                m_buf[pl.ds(r * tok, tok), :],
                w_pair[(c + j) % 2, pl.ds(pl.multiple_of(n * nt, nt), nt), :],
                (((1,), (1,)), ((), ())),
                preferred_element_type=F32,
            )
            cols = pl.ds(pl.multiple_of(n * nt, nt), nt)

            @pl.when(j == 0)
            def _():
                i_keep[r, :, cols] = part

            @pl.when(j == 1)
            def _():
                i_send[r, :, cols] = part.astype(BF16)

            return carry

        lax.fori_loop(0, 4, one, 0)
        return remote(i_send.at[r], i_recv.at[r], core_peer)

    def finished(r, copy):
        copy.wait_recv()

        def one(t, carry):
            part = pl.ds(pl.multiple_of(t * 64, 64), 64)
            o_fin[r, part, :] = (i_keep[r, part, :] + i_recv[r, part, :].astype(F32)).astype(BF16)
            return carry

        lax.fori_loop(0, tok // 64, one, 0)

    def out_columns(ychip):
        return pl.ds(pl.multiple_of(ychip * 2 * blk + c * blk, blk), blk)

    out_stores, out_in = [], []

    def spread(src, ychip):
        out_stores.append(local(src, grad_out.at[:, out_columns(ychip)]))
        out_in.append(remote(src, grad_out.at[:, out_columns(ychip)], core_peer))

    in_m.wait()
    in_w.wait()
    pair.wait_recv()
    p0 = partial_terms(0)
    up_b.wait_recv()
    p3 = partial_terms(3)
    dn_a.wait_recv()
    p1 = partial_terms(1)
    o_in = {}
    finished(3, p3)
    o_in[1] = remote(o_fin.at[3], o_recv.at[0], at_y(-1))
    finished(1, p1)
    o_in[3] = remote(o_fin.at[1], o_recv.at[2], at_y(1))
    finished(0, p0)
    spread(o_fin.at[0], y)

    fwd_up.wait_recv()
    fwd_dn.wait_recv()
    p2 = partial_terms(2)

    hn = hw // 4
    rs_in, v_in = [], []
    for k in range(nk):
        in_f[k].wait()
        shared = []
        for slot in (3, 1, 2):
            f_in[k, slot].wait_recv()
            shared.append(remote(f_buf.at[k, f_rows(slot)], f_buf.at[k, f_rows(slot)], core_peer))
        for copy in shared:
            copy.wait_recv()

        def turn(t, carry):
            part = pl.ds(pl.multiple_of(t * tok, tok), tok)
            ft_buf[:, part] = f_buf[k, part, :].T
            return carry

        lax.fori_loop(0, NY, turn, 0)

        def one(n, carry):
            cols = pl.ds(pl.multiple_of(n * hn, hn), hn)
            part = jnp.dot(ft_buf[...], m_buf[:, cols], preferred_element_type=F32)
            if k < nq:
                rs_send[k, :, cols] = part.astype(BF16)
            else:
                g_own[:, cols] = part
            return carry

        lax.fori_loop(0, 4, one, 0)
        if k < nq:
            rs_in.append(remote(rs_send.at[k], rs_recv.at[k], z_peer))
            if k == 0:
                finished(2, p2)
                o_in[2] = remote(o_fin.at[2], o_recv.at[1], at_y(2))
            continue
        q = k - nq
        if q == 0:
            in_v.wait()
        rs_in[q].wait_recv()

        def move(t, carry):
            part = pl.ds(pl.multiple_of(t * 32, 32), 32)
            own = pl.ds(pl.multiple_of(q * sub + t * 32, 32), 32)
            grad = (g_own[part, :] + rs_recv[q, part, :].astype(F32)) * (1.0 / (NY * 2 * tok))
            vel = momentum_keep * v_own[own, :] + grad
            v_own[own, :] = vel
            v_send[q, part, :] = vel.astype(BF16)
            return carry

        lax.fori_loop(0, sub // 32, move, 0)
        v_in.append(remote(v_send.at[q], v_peer.at[q], peer))

    def spread_arrived():
        for slot in (1, 3, 2):
            o_in[slot].wait_recv()
            spread(o_recv.at[slot - 1], (y + slot) % NY)

    if bit < 2:
        spread_arrived()
    rate = rate_ref[0]
    in_wf.wait()
    w_swap.wait_recv()
    results = []
    for q in range(nq):
        v_in[q].wait_recv()

        def final(t, carry):
            part = pl.ds(pl.multiple_of(t * 32, 32), 32)
            own = pl.ds(pl.multiple_of(q * sub + t * 32, 32), 32)
            vel = 0.5 * (v_own[own, :] + v_peer[q, part, :].astype(F32))
            v_own[own, :] = vel
            w_own[own, :] = 0.5 * (w_own[own, :] + w_peer[own, :].astype(F32)) - rate * vel
            return carry

        lax.fori_loop(0, sub // 32, final, 0)
        own = pl.ds(q * sub, sub)
        results.append(local(v_own.at[own], v_out.at[own]))
        results.append(local(w_own.at[own], w_out.at[own]))
    if bit >= 2:
        spread_arrived()
    for copy in out_in:
        copy.wait_recv()
    for copy in pending:
        copy.wait_send()
    for copy in results + out_stores:
        copy.wait()


def make_call(bit, tok, width, blk, hw, subs=4):
    sub = 2 * blk // subs
    any_space = pl.BlockSpec(memory_space=pl.ANY)
    flops = 4 * tok * width * hw
    return pl.pallas_call(
        functools.partial(body, bit),
        name=f"pod_step_{bit}",
        out_shape=(
            jax.ShapeDtypeStruct((tok, width), BF16),
            jax.ShapeDtypeStruct((blk, hw), F32),
            jax.ShapeDtypeStruct((blk, hw), F32),
        ),
        in_specs=[pl.BlockSpec(memory_space=pltpu.SMEM)] + [any_space] * 5,
        out_specs=(any_space, any_space, any_space),
        scratch_shapes=[
            pltpu.VMEM((NY * tok, hw), BF16),
            pltpu.VMEM((subs, NY * tok, sub), BF16),
            pltpu.VMEM((sub, NY * tok), BF16),
            pltpu.VMEM((2, blk, hw), BF16),
            pltpu.VMEM((subs // 2, sub, hw), BF16),
            pltpu.VMEM((subs // 2, sub, hw), BF16),
            pltpu.VMEM((sub, hw), F32),
            pltpu.VMEM((blk, hw), F32),
            pltpu.VMEM((blk, hw), F32),
            pltpu.VMEM((blk, hw), BF16),
            pltpu.VMEM((subs // 2, sub, hw), BF16),
            pltpu.VMEM((subs // 2, sub, hw), BF16),
            pltpu.VMEM((NY, tok, blk), F32),
            pltpu.VMEM((NY, tok, blk), BF16),
            pltpu.VMEM((NY, tok, blk), BF16),
            pltpu.VMEM((NY, tok, blk), BF16),
            pltpu.VMEM((NY - 1, tok, blk), BF16),
            pltpu.SemaphoreType.DMA((64,)),
            pltpu.SemaphoreType.DMA((96,)),
            pltpu.SemaphoreType.DMA((96,)),
        ],
        compiler_params=pltpu.CompilerParams(
            collective_id=bit, has_side_effects=True, vmem_limit_bytes=60 * 1024 * 1024
        ),
        cost_estimate=pl.CostEstimate(flops=flops, bytes_accessed=32 << 20, transcendentals=0),
    )


def on_device(step_index, token_ids, features, cotangent, weight, momentum):
    feat = features[0]
    tok, width = feat.shape
    blk, hw = weight.shape[1:]
    keep_mask = (token_ids[0] != pad_token)[:, None]
    masked = jnp.where(keep_mask, cotangent[0], jnp.zeros_like(cotangent[0]))
    whalf = weight[0].astype(BF16)
    rate = peak_rate * (step_index + 1).astype(F32) / warm_steps
    bit_count = lax.axis_size("outer").bit_length() - 1
    calls = [make_call(b, tok, width, blk, hw) for b in range(bit_count)]
    operands = (rate[None], feat, masked, whalf, weight[0], momentum[0])
    input_grad, new_master, new_velocity = lax.switch(
        step_index % bit_count, [lambda *a, call=call: call(*a) for call in calls], *operands
    )
    return (input_grad[None], new_master[None], new_velocity[None])


def solution(mesh):
    placed = (
        P(),
        P("outer", "dp"),
        P("outer", "dp", None),
        P("outer", "dp", "mp"),
        P("outer", "dp", "mp"),
        P("outer", "dp", "mp"),
    )
    return jax.shard_map(
        on_device,
        mesh=mesh,
        in_specs=placed,
        out_specs=(P("outer", "dp", None), P("outer", "dp", "mp"), P("outer", "dp", "mp")),
        check_vma=False,
    )
```

```python
import functools

import jax
import jax.numpy as jnp
from jax import lax
from jax.experimental import pallas as pl
from jax.experimental.pallas import tpu as pltpu
from jax.sharding import PartitionSpec as P

pad_token = 128004
peak_rate = 0.1
warm_steps = 4096.0
momentum_keep = 0.9

MESH = pl.DeviceIdType.MESH
BF16 = jnp.bfloat16
F32 = jnp.float32
NY = 4
NX = 4


def body(
    bit,
    rate_ref,
    ids,
    feat,
    cot,
    weight,
    momentum,
    grad_out,
    w_out,
    v_out,
    m_buf,
    f_buf,
    ft_buf,
    w_pair,
    rs_send,
    rs_recv,
    g_own,
    w_own,
    v_own,
    w_peer,
    v_send,
    v_peer,
    i_keep,
    i_send,
    i_recv,
    o_fin,
    o_recv,
    loc,
    snd,
    rcv,
):
    outer, dp, c = lax.axis_index("outer"), lax.axis_index("dp"), lax.axis_index("mp")
    x, zh = outer // NX, outer % NX
    y, zl = dp // 2, dp % 2
    tok, hw = cot.shape
    half = tok // 2
    blk = weight.shape[0]
    nk = f_buf.shape[0]
    sub = f_buf.shape[2]
    nq = nk // 2

    def at_y(step):
        return (outer, ((y + step + NY) % NY) * 2 + zl, c)

    z_peer = (outer, y * 2 + 1 - zl, c)
    core_peer = (outer, dp, 1 - c)
    if bit == 0:
        other = x * 4 + zh + 1 - 2 * (zh % 2)
    elif bit == 1:
        other = x * 4 + (zh + 2) % 4
    elif bit == 2:
        other = (x + 1 - 2 * (x % 2)) * 4 + zh
    else:
        other = ((x + 2) % 4) * 4 + zh
    peer = (other, dp, c)

    count = {"loc": 0, "rem": 0}

    def local(src, dst):
        i = count["loc"]
        count["loc"] += 1
        copy = pltpu.make_async_copy(src, dst, loc.at[i])
        copy.start()
        return copy

    pending = []

    def remote(src, dst, to):
        i = count["rem"]
        count["rem"] += 1
        copy = pltpu.make_async_remote_copy(
            src_ref=src,
            dst_ref=dst,
            send_sem=snd.at[i],
            recv_sem=rcv.at[i],
            device_id=to,
            device_id_type=MESH,
        )
        copy.start()
        pending.append(copy)
        return copy

    in_m = local(cot, m_buf.at[pl.ds(0, tok)])
    in_wf = local(weight, w_own)

    barrier = pltpu.get_barrier_semaphore()
    partners = (at_y(1), at_y(-1), at_y(2), z_peer, core_peer, peer)
    for to in partners:
        pl.semaphore_signal(barrier, inc=1, device_id=to, device_id_type=MESH)
    in_m.wait()
    lanes = ids.shape[1]
    for t in range(tok // lanes):
        part = pl.ds(t * lanes, lanes)
        keep = jnp.where(ids[pl.ds(t, 1), :] == pad_token, 0.0, 1.0)
        keep = jnp.broadcast_to(keep, (lanes, lanes)).T.astype(BF16)
        for n in range(hw // lanes):
            cols = pl.ds(n * lanes, lanes)
            m_buf[part, cols] = m_buf[part, cols] * keep
    in_wf.wait()

    def halve(t, carry):
        part = pl.ds(pl.multiple_of(t * 32, 32), 32)
        w_pair[zl, part, :] = w_own[part, :].astype(BF16)
        return carry

    lax.fori_loop(0, blk // 32, halve, 0)
    pl.semaphore_wait(barrier, len(partners))

    def rows(r, part):
        return pl.ds(r * tok + part * half, half)

    up_a = remote(m_buf.at[rows(0, 0)], m_buf.at[rows(3, 0)], at_y(1))
    dn_b = remote(m_buf.at[rows(0, 1)], m_buf.at[rows(1, 1)], at_y(-1))
    up_b = remote(m_buf.at[rows(0, 1)], m_buf.at[rows(3, 1)], at_y(1))
    dn_a = remote(m_buf.at[rows(0, 0)], m_buf.at[rows(1, 0)], at_y(-1))
    pair = remote(w_pair.at[zl], w_pair.at[zl], z_peer)
    w_swap = remote(w_pair.at[zl], w_peer, peer)

    def columns(ychip, k):
        j = (1 - zl) if k < nq else zl
        return pl.ds(pl.multiple_of(ychip * 2 * blk + j * blk + (k % nq) * sub, sub), sub)

    in_f = [local(feat.at[:, columns(y, k)], f_buf.at[k, pl.ds(0, tok)]) for k in range(nk)]
    in_v = local(momentum, v_own)

    up_a.wait_recv()
    fwd_up = remote(m_buf.at[rows(3, 0)], m_buf.at[rows(2, 0)], at_y(1))
    dn_b.wait_recv()
    fwd_dn = remote(m_buf.at[rows(1, 1)], m_buf.at[rows(2, 1)], at_y(-1))

    mine = pl.ds(pl.multiple_of(c * half, half), half)

    def f_rows(r):
        return pl.ds(pl.multiple_of(r * tok + c * half, half), half)

    f_in = {}
    for k in range(nk):
        for step, slot in ((1, 3), (-1, 1), (2, 2)):
            f_in[k, slot] = remote(
                feat.at[mine, columns((y + step + NY) % NY, k)],
                f_buf.at[k, f_rows(slot)],
                at_y(step),
            )

    nt = blk // 2

    def partial_terms(r):
        def one(t, carry):
            j, n = t // 2, t % 2
            part = lax.dot_general(
                m_buf[pl.ds(r * tok, tok), :],
                w_pair[(c + j) % 2, pl.ds(pl.multiple_of(n * nt, nt), nt), :],
                (((1,), (1,)), ((), ())),
                preferred_element_type=F32,
            )
            cols = pl.ds(pl.multiple_of(n * nt, nt), nt)

            @pl.when(j == 0)
            def _():
                i_keep[r, :, cols] = part

            @pl.when(j == 1)
            def _():
                i_send[r, :, cols] = part.astype(BF16)

            return carry

        lax.fori_loop(0, 4, one, 0)
        return remote(i_send.at[r], i_recv.at[r], core_peer)

    def finished(r, copy):
        copy.wait_recv()

        def one(t, carry):
            part = pl.ds(pl.multiple_of(t * 64, 64), 64)
            o_fin[r, part, :] = (i_keep[r, part, :] + i_recv[r, part, :].astype(F32)).astype(BF16)
            return carry

        lax.fori_loop(0, tok // 64, one, 0)

    def out_columns(ychip):
        return pl.ds(pl.multiple_of(ychip * 2 * blk + c * blk, blk), blk)

    out_stores, out_in = [], []

    def spread(src, ychip):
        out_stores.append(local(src, grad_out.at[:, out_columns(ychip)]))
        out_in.append(remote(src, grad_out.at[:, out_columns(ychip)], core_peer))

    pair.wait_recv()
    p0 = partial_terms(0)
    up_b.wait_recv()
    p3 = partial_terms(3)
    dn_a.wait_recv()
    p1 = partial_terms(1)
    o_in = {}
    finished(3, p3)
    o_in[1] = remote(o_fin.at[3], o_recv.at[0], at_y(-1))
    finished(1, p1)
    o_in[3] = remote(o_fin.at[1], o_recv.at[2], at_y(1))
    finished(0, p0)
    spread(o_fin.at[0], y)

    fwd_up.wait_recv()
    fwd_dn.wait_recv()
    p2 = partial_terms(2)

    hn = hw // 4
    rs_in, v_in = [], []
    for k in range(nk):
        in_f[k].wait()
        shared = []
        for slot in (3, 1, 2):
            f_in[k, slot].wait_recv()
            shared.append(remote(f_buf.at[k, f_rows(slot)], f_buf.at[k, f_rows(slot)], core_peer))
        for copy in shared:
            copy.wait_recv()

        def turn(t, carry):
            part = pl.ds(pl.multiple_of(t * tok, tok), tok)
            ft_buf[:, part] = f_buf[k, part, :].T
            return carry

        lax.fori_loop(0, NY, turn, 0)

        def one(n, carry):
            cols = pl.ds(pl.multiple_of(n * hn, hn), hn)
            part = jnp.dot(ft_buf[...], m_buf[:, cols], preferred_element_type=F32)
            if k < nq:
                rs_send[k, :, cols] = part.astype(BF16)
            else:
                g_own[:, cols] = part
            return carry

        lax.fori_loop(0, 4, one, 0)
        if k < nq:
            rs_in.append(remote(rs_send.at[k], rs_recv.at[k], z_peer))
            if k == 0:
                finished(2, p2)
                o_in[2] = remote(o_fin.at[2], o_recv.at[1], at_y(2))
            continue
        q = k - nq
        if q == 0:
            in_v.wait()
        rs_in[q].wait_recv()

        def move(t, carry):
            part = pl.ds(pl.multiple_of(t * 32, 32), 32)
            own = pl.ds(pl.multiple_of(q * sub + t * 32, 32), 32)
            grad = (g_own[part, :] + rs_recv[q, part, :].astype(F32)) * (1.0 / (NY * 2 * tok))
            vel = momentum_keep * v_own[own, :] + grad
            v_own[own, :] = vel
            v_send[q, part, :] = vel.astype(BF16)
            return carry

        lax.fori_loop(0, sub // 32, move, 0)
        v_in.append(remote(v_send.at[q], v_peer.at[q], peer))

    def spread_arrived():
        for slot in (1, 3, 2):
            o_in[slot].wait_recv()
            spread(o_recv.at[slot - 1], (y + slot) % NY)

    if bit < 2:
        spread_arrived()
    rate = rate_ref[0]
    w_swap.wait_recv()
    results = []
    for q in range(nq):
        v_in[q].wait_recv()

        def final(t, carry):
            part = pl.ds(pl.multiple_of(t * 32, 32), 32)
            own = pl.ds(pl.multiple_of(q * sub + t * 32, 32), 32)
            vel = 0.5 * (v_own[own, :] + v_peer[q, part, :].astype(F32))
            v_own[own, :] = vel
            w_own[own, :] = 0.5 * (w_own[own, :] + w_peer[own, :].astype(F32)) - rate * vel
            return carry

        lax.fori_loop(0, sub // 32, final, 0)
        own = pl.ds(q * sub, sub)
        results.append(local(v_own.at[own], v_out.at[own]))
        results.append(local(w_own.at[own], w_out.at[own]))
    if bit >= 2:
        spread_arrived()
    for copy in out_in:
        copy.wait_recv()
    for copy in pending:
        copy.wait_send()
    for copy in results + out_stores:
        copy.wait()


def make_call(bit, tok, width, blk, hw, subs=8):
    sub = 2 * blk // subs
    any_space = pl.BlockSpec(memory_space=pl.ANY)
    flops = 4 * tok * width * hw
    return pl.pallas_call(
        functools.partial(body, bit),
        name=f"pod_step_{bit}",
        out_shape=(
            pltpu.VMEM((tok, width), BF16),
            pltpu.VMEM((blk, hw), F32),
            pltpu.VMEM((blk, hw), F32),
        ),
        in_specs=[pl.BlockSpec(memory_space=pltpu.SMEM)] + [pl.BlockSpec(memory_space=pltpu.VMEM)] + [any_space] * 4,
        out_specs=(pl.BlockSpec(memory_space=pltpu.VMEM),) * 3,
        scratch_shapes=[
            pltpu.VMEM((NY * tok, hw), BF16),
            pltpu.VMEM((subs, NY * tok, sub), BF16),
            pltpu.VMEM((sub, NY * tok), BF16),
            pltpu.VMEM((2, blk, hw), BF16),
            pltpu.VMEM((subs // 2, sub, hw), BF16),
            pltpu.VMEM((subs // 2, sub, hw), BF16),
            pltpu.VMEM((sub, hw), F32),
            pltpu.VMEM((blk, hw), F32),
            pltpu.VMEM((blk, hw), F32),
            pltpu.VMEM((blk, hw), BF16),
            pltpu.VMEM((subs // 2, sub, hw), BF16),
            pltpu.VMEM((subs // 2, sub, hw), BF16),
            pltpu.VMEM((NY, tok, blk), F32),
            pltpu.VMEM((NY, tok, blk), BF16),
            pltpu.VMEM((NY, tok, blk), BF16),
            pltpu.VMEM((NY, tok, blk), BF16),
            pltpu.VMEM((NY - 1, tok, blk), BF16),
            pltpu.SemaphoreType.DMA((64,)),
            pltpu.SemaphoreType.DMA((96,)),
            pltpu.SemaphoreType.DMA((96,)),
        ],
        compiler_params=pltpu.CompilerParams(
            collective_id=bit, has_side_effects=True, vmem_limit_bytes=50 * 1024 * 1024
        ),
        cost_estimate=pl.CostEstimate(flops=flops, bytes_accessed=32 << 20, transcendentals=0),
    )


def store(*refs):
    sems = refs[-1]
    copies = [pltpu.make_async_copy(refs[i], refs[3 + i], sems.at[i]) for i in range(3)]
    for copy in copies:
        copy.start()
    for copy in copies:
        copy.wait()


def stored(results):
    return pl.pallas_call(
        store,
        name="store",
        out_shape=tuple(jax.ShapeDtypeStruct(r.shape, r.dtype) for r in results),
        in_specs=[pl.BlockSpec(memory_space=pltpu.VMEM)] * 3,
        out_specs=(pl.BlockSpec(memory_space=pltpu.HBM),) * 3,
        scratch_shapes=[pltpu.SemaphoreType.DMA((3,))],
        compiler_params=pltpu.CompilerParams(vmem_limit_bytes=40 * 1024 * 1024),
    )(*results)


def on_device(step_index, token_ids, features, cotangent, weight, momentum):
    feat = features[0]
    tok, width = feat.shape
    blk, hw = weight.shape[1:]
    ids = token_ids.reshape(tok // 128, 128)
    rate = peak_rate * (step_index + 1).astype(F32) / warm_steps
    bit_count = lax.axis_size("outer").bit_length() - 1
    calls = [make_call(b, tok, width, blk, hw) for b in range(bit_count)]
    operands = (rate[None], ids, feat, cotangent[0], weight[0], momentum[0])
    input_grad, new_master, new_velocity = lax.switch(
        step_index % bit_count, [lambda *a, call=call: stored(call(*a)) for call in calls], *operands
    )
    return (input_grad[None], new_master[None], new_velocity[None])


def solution(mesh):
    placed = (
        P(),
        P("outer", "dp"),
        P("outer", "dp", None),
        P("outer", "dp", "mp"),
        P("outer", "dp", "mp"),
        P("outer", "dp", "mp"),
    )
    return jax.shard_map(
        on_device,
        mesh=mesh,
        in_specs=placed,
        out_specs=(P("outer", "dp", None), P("outer", "dp", "mp"), P("outer", "dp", "mp")),
        check_vma=False,
    )
```
